32 devices in a mesh: grp: 2 (over y), row: 4 (over z), col: 2 (over x), pole: 2 (over core).
Axes of the slice: x: 2, y: 2, z: 4, core: 2. Of those that a mesh axis runs over, the one named last changes fastest.
Arguments:
- inverse_front: bfloat16 [4, 2, 8192, 4096], P(('grp', 'pole'), None, 'row', 'col'), parts along dimension 0, may hold values from -6 to 6
- tile_mask: int32 [128, 32], P(('grp', 'row'), 'col'), parts along dimension 0, may hold values 0 or 1
- lower_panel: bfloat16 [2, 4, 2, 256, 4096], P(None, ('grp', 'pole'), None, 'row', 'col'), parts along dimension 1, may hold values from -0.09375 to 0.09375
- upper_panel: bfloat16 [2, 4, 2, 256, 8192], P(None, ('grp', 'pole'), None, 'col', 'row'), parts along dimension 1, may hold values from -0.0625 to 0.0625
- pivots: float32 [2, 4, 256], P(None, ('grp', 'pole')), parts along dimension 1, may hold values from 0.01 to 0.1
- pole_weight: float32 [2, 128], P(None, 'grp'), parts along dimension 1, may hold values from -4 to 4
- pole_slot: int32 [4], P('grp'), parts along dimension 0, may hold values from 0 to 63
- supernode: int32 [1024], P('grp'), parts along dimension 0, may hold values from 0 to 127, never falling along the last dimension, each value on 1 to 64 neighbouring positions
Outputs:
- updated_front: bfloat16 [4, 2, 8192, 4096], P(('grp', 'pole'), None, 'row', 'col'), parts along dimension 0
- density: float32 [4, 256, 256], P('grp', None, 'col'), parts along dimension 0
The draws below stay inside these ranges and needn't reach their ends.
There are 2 independent parts, one for each index of `grp`. The reference program is written for one: setup_inputs(seed, part) draws one part's arguments, and reference() takes and returns one part's arrays. A program takes and returns all parts, laid end to end along the dimension named above; each array names one. Nothing has to cross between parts.
Inputs may be any that keep to these rules, and one draw needn't show every extreme that they name: `tile_mask`: 1 marks a present tile of 128 x 128 entries. `pole_slot`: each slot names one pole of the table. Never falling along the 512 columns; each supernode spans at most 64 columns.
All inputs are finite; a program needn't handle non-finite values. No bound on the sum of `tile_mask` on one device may be relied on, other than what follows from the above.
Results may differ from the reference program's by a relative error of at most 0.035.
Values may be sent and summed in bfloat16 or wider, within the bound.
No kernel may reach another device: no remote copies, remote signals or barrier semaphores. Data moves between devices by JAX's collectives and lax.ppermute only.
A program may use at most 192 MiB of HBM per device.

```python
import math
import jax
import jax.numpy as jnp
import numpy as np

FRONT_ROWS = 8192
FRONT_COLS = 4096
PANEL = 256
TILE = 128
POLE_TABLE = 64
POLES = 2
N_ROW = 4
N_COL = 2


def touch_ends(array, key, low, top_value):
    extent = array.shape
    place = [jax.random.randint(jax.random.fold_in(key, axis), (), 0, extent[axis]) for axis in range(len(extent))]
    array = array.at[tuple(place)].set(low)
    longest = extent.index(max(extent))
    place[longest] = (place[longest] + 1) % extent[longest]
    return array.at[tuple(place)].set(top_value)


def block_scale(stream_key, extent, split, smallest, top_value):
    loudness, own = 1.0, jax.random.fold_in(stream_key, 6)
    for axis_at, blocks in split:
        steps = jnp.exp(jax.random.uniform(jax.random.fold_in(own, axis_at), (blocks,), jnp.float32, smallest / len(split), top_value / len(split)))
        loudness = loudness * jnp.repeat(steps, extent[axis_at] // blocks).reshape([-1 if axis == axis_at else 1 for axis in range(len(extent))])
    return loudness


def profile(number_of, total, most, lean):
    loads = [(1 << 20) // math.isqrt(grade ** lean) + 1 for grade in range(2, number_of + 1)]
    rest, holding = total - most - (number_of - 1), [1] * (number_of - 1)
    while rest > 0:
        movable = [i for i in range(number_of - 1) if holding[i] < most]
        pool, remaining = sum([loads[i] for i in movable]), rest
        for i in movable:
            extra = min(most - holding[i], max(1, remaining * loads[i] // pool), rest)
            holding[i] = holding[i] + extra
            rest = rest - extra
    return np.array([most] + holding)


def uneven_parts(rng, number_of, total, limit, lean):
    if number_of == 2:
        one = jax.random.randint(rng, (), max(1, total - limit), min(limit, total - 1) + 1)
        return jnp.stack([one, total - one])
    sizes = jnp.asarray(profile(number_of, total, limit, lean), jnp.int32)
    couples = (number_of - 1) // 2
    source_of, sink = sizes[1:1 + 2 * couples:2], sizes[2:2 + 2 * couples:2]
    room = jnp.minimum(source_of - 1, limit - sink)
    passed = jax.random.randint(jax.random.fold_in(rng, 1), (couples,), 0, 1 << 20) % (room + 1)
    sizes = sizes.at[1:1 + 2 * couples:2].set(source_of - passed).at[2:2 + 2 * couples:2].set(sink + passed)
    return sizes[jax.random.permutation(jax.random.fold_in(rng, 2), number_of)]


def scatter_about(key, extent, deviation, reach, pieces=(), kind=jnp.bfloat16):
    entries = deviation * jax.random.normal(key, extent, jnp.float32)
    if pieces:
        entries = entries * block_scale(key, extent, pieces, -0.22, 0.18)
    return jnp.clip(entries, -reach, reach).astype(kind)


def setup_inputs(seed: int = 0, part: int = 0) -> dict:
    seeds = jax.random.split(jax.random.key(seed), 9)
    part_splits = jax.random.split(jax.random.fold_in(seeds[8], part), 9)
    return {
        "inverse_front": scatter_about(part_splits[0], (POLES, 2, FRONT_ROWS, FRONT_COLS), 1.0, 6.0, ((0, 2), (2, 4), (3, 2))),
        "tile_mask": touch_ends((jax.random.randint(part_splits[1], (FRONT_ROWS // TILE, FRONT_COLS // TILE), 0, 4) < 3).astype(jnp.int32), jax.random.fold_in(part_splits[1], 1), 0, 1),
        "lower_panel": scatter_about(part_splits[2], (2, POLES, 2, PANEL, FRONT_COLS), FRONT_COLS ** -0.5, 0.09375, ((1, 2), (3, 4), (4, 2))),
        "upper_panel": scatter_about(part_splits[3], (2, POLES, 2, PANEL, FRONT_ROWS), FRONT_ROWS ** -0.5, 0.0625, ((1, 2), (3, 2), (4, 4))),
        "pivots": jnp.clip(jnp.exp(math.log(0.1) - 2.3025851 * jax.random.uniform(part_splits[4], (2, POLES, PANEL), jnp.float32) ** block_scale(part_splits[4], (2, POLES, PANEL), ((1, 2),), -0.2, 0.2)), 0.01, 0.1),
        "pole_weight": scatter_about(part_splits[5], (2, POLE_TABLE), 1.0, 4.0, (), jnp.float32),
        "pole_slot": jax.random.randint(part_splits[6], (POLES,), 0, POLE_TABLE).astype(jnp.int32),
        "supernode": jnp.searchsorted(jnp.cumsum(uneven_parts(part_splits[7], PANEL // 2, 2 * PANEL, PANEL // 4, 0)), jnp.arange(2 * PANEL), side="right").astype(jnp.int32),
    }


def complex_dot(left_real, left_imag, right_real, right_imag):
    def single(one, other):
        return jnp.dot(one, other, preferred_element_type=jnp.float32)
    real_part = single(left_real, right_real) - single(left_imag, right_imag)
    imag_part = single(left_real, right_imag) + single(left_imag, right_real)
    return real_part, imag_part


def reference(inverse_front, tile_mask, lower_panel, upper_panel, pivots, pole_weight, pole_slot, supernode):
    cell_mask = jnp.repeat(jnp.repeat(tile_mask, TILE, axis=0), TILE, axis=1).astype(jnp.float32)
    cell_narrow = cell_mask.astype(jnp.bfloat16)
    row_block = FRONT_ROWS // N_ROW
    col_block = FRONT_COLS // N_COL
    raw_density = [jnp.zeros((PANEL, PANEL), jnp.float32), jnp.zeros((PANEL, PANEL), jnp.float32)]
    fronts = []
    for slot_index in range(POLES):
        front_real = inverse_front[slot_index, 0]
        front_imag = inverse_front[slot_index, 1]
        weight_real = pole_weight[0, pole_slot[slot_index]]
        weight_imag = pole_weight[1, pole_slot[slot_index]]
        for panel_index in range(2):
            masked_real = front_real * cell_narrow
            masked_imag = front_imag * cell_narrow
            lower_real = lower_panel[panel_index, slot_index, 0]
            lower_imag = lower_panel[panel_index, slot_index, 1]
            upper_real = upper_panel[panel_index, slot_index, 0]
            upper_imag = upper_panel[panel_index, slot_index, 1]
            x_real = jnp.zeros((FRONT_ROWS, PANEL), jnp.float32)
            x_imag = jnp.zeros((FRONT_ROWS, PANEL), jnp.float32)
            for col_index in range(N_COL):
                lo_col = col_index * col_block
                hi_col = lo_col + col_block
                part_real, part_imag = complex_dot(masked_real[:, lo_col:hi_col], masked_imag[:, lo_col:hi_col], lower_real[:, lo_col:hi_col].T, lower_imag[:, lo_col:hi_col].T)
                x_real = x_real + (-part_real).astype(jnp.bfloat16).astype(jnp.float32)
                x_imag = x_imag + (-part_imag).astype(jnp.bfloat16).astype(jnp.float32)
            x_real = x_real.astype(jnp.bfloat16)
            x_imag = x_imag.astype(jnp.bfloat16)
            y_real = jnp.zeros((PANEL, FRONT_COLS), jnp.float32)
            y_imag = jnp.zeros((PANEL, FRONT_COLS), jnp.float32)
            for row_index in range(N_ROW):
                lo_row = row_index * row_block
                hi_row = lo_row + row_block
                part_real, part_imag = complex_dot(upper_real[:, lo_row:hi_row], upper_imag[:, lo_row:hi_row], masked_real[lo_row:hi_row], masked_imag[lo_row:hi_row])
                y_real = y_real + (-part_real).astype(jnp.bfloat16).astype(jnp.float32)
                y_imag = y_imag + (-part_imag).astype(jnp.bfloat16).astype(jnp.float32)
            y_real = y_real.astype(jnp.bfloat16)
            y_imag = y_imag.astype(jnp.bfloat16)
            g_real, g_imag = complex_dot(upper_real, upper_imag, x_real, x_imag)
            raw_density[panel_index] = raw_density[panel_index] - weight_real * g_real + weight_imag * g_imag
            column_scale = pivots[panel_index, slot_index][None, :]
            scaled_real = (x_real.astype(jnp.float32) * column_scale).astype(jnp.bfloat16)
            scaled_imag = (x_imag.astype(jnp.float32) * column_scale).astype(jnp.bfloat16)
            update_real, update_imag = complex_dot(scaled_real, scaled_imag, y_real, y_imag)
            front_real = (front_real.astype(jnp.float32) + cell_mask * update_real).astype(jnp.bfloat16)
            front_imag = (front_imag.astype(jnp.float32) + cell_mask * update_imag).astype(jnp.bfloat16)
        fronts.append(jnp.stack([front_real, front_imag]))
    results = []
    for panel_index in range(2):
        labels = supernode[panel_index * PANEL:(panel_index + 1) * PANEL]
        same_node = labels[:, None] == labels[None, :]
        results.append(jnp.where(same_node, raw_density[panel_index], jnp.zeros((), jnp.float32)))
    return jnp.stack(fronts), jnp.stack(results)
```

```python
import functools

import jax
import jax.numpy as jnp
from jax import lax
from jax.experimental import pallas as pl
from jax.experimental.pallas import tpu as pltpu
from jax.sharding import PartitionSpec as P

F32 = jnp.float32
BF16 = jnp.bfloat16
CONTRACT_LAST = (((1,), (1,)), ((), ()))
VMEM_LIMIT = 56 << 20


def whole(shape):
    return pl.BlockSpec(
        shape, lambda *_: (0,) * len(shape), pipeline_mode=pl.Buffered(1)
    )


def call(kernel, grid, scalars, operands, outs, scratch, flops, aliases=None):
    moved = sum(a.size * a.dtype.itemsize for a, _ in operands)
    moved += sum(o.size * o.dtype.itemsize for o, _ in outs)
    shapes = [o for o, _ in outs]
    specs = [s for _, s in outs]
    return pl.pallas_call(
        kernel,
        grid_spec=pltpu.PrefetchScalarGridSpec(
            num_scalar_prefetch=len(scalars),
            grid=grid,
            in_specs=[s for _, s in operands],
            out_specs=specs,
            scratch_shapes=scratch,
        ),
        out_shape=shapes,
        input_output_aliases=aliases or {},
        compiler_params=pltpu.CompilerParams(vmem_limit_bytes=VMEM_LIMIT),
        cost_estimate=pl.CostEstimate(
            flops=flops, bytes_accessed=moved, transcendentals=0
        ),
    )(*scalars, *[a for a, _ in operands])


def assemble(owners, slots, full):
    share = slots[0].shape[1]
    width = share * len(slots)
    for k, slot in enumerate(slots):
        start = pl.multiple_of(owners[k] * share, share)
        for part in range(2):
            full[pl.ds(part * width + start, share), :] = slot[part]


def masked_tiles(mask, source, target, tile, row_tile, col_tile):
    rows, cols = source.shape[1:]
    for part in range(2):
        for i in range(rows // tile):
            for k in range(cols // tile):
                keep = mask[row_tile + i, col_tile + k] != 0
                at = (
                    part,
                    slice(i * tile, (i + 1) * tile),
                    slice(k * tile, (k + 1) * tile),
                )
                block = source[at]
                target[at] = jnp.where(keep, block, jnp.zeros_like(block))


def store_y(upper, masked, y_ref):
    width = upper.shape[0] // 2
    by_real = jnp.dot(upper[...], masked[0], preferred_element_type=F32)
    by_imag = jnp.dot(upper[...], masked[1], preferred_element_type=F32)
    y_ref[0] = (by_imag[width:] - by_real[:width]).astype(BF16)
    y_ref[1] = (-(by_imag[:width] + by_real[width:])).astype(BF16)


def y_kernel(mask, owners, front, *rest, tile, first):
    *slots, y_ref, masked, upper = rest

    @pl.when(pl.program_id(0) == 0)
    def _():
        assemble(owners, slots, upper)

    step = first + pl.program_id(0)
    masked_tiles(mask, front, masked, tile, 0, step * (front.shape[2] // tile))
    store_y(upper, masked, y_ref)


def y_part(front, mask, owners, slots, chunk, chunks, tile):
    _, rows, cols = front.shape
    width = slots[0].shape[1] * len(slots)
    span = cols // chunks
    block = min(256, span)
    first = chunk * (span // block)
    return call(
        functools.partial(y_kernel, tile=tile, first=first),
        (span // block,),
        (mask, owners),
        [(front, pl.BlockSpec((2, rows, block), lambda j, *_: (0, 0, first + j)))]
        + [(s, whole(s.shape)) for s in slots],
        [
            (
                jax.ShapeDtypeStruct((2, width, span), BF16),
                pl.BlockSpec((2, width, block), lambda j, *_: (0, 0, j)),
            )
        ],
        [pltpu.VMEM((2, rows, block), BF16), pltpu.VMEM((2 * width, rows), BF16)],
        8 * width * rows * span,
    )[0]


def x_kernel(mask, owners, front, *rest, tile, first):
    *slots, x_ref, masked, lower = rest

    @pl.when(pl.program_id(0) == 0)
    def _():
        assemble(owners, slots, lower)

    step = first + pl.program_id(0)
    masked_tiles(mask, front, masked, tile, step * (front.shape[1] // tile), 0)
    width = lower.shape[0] // 2
    by_real = lax.dot_general(
        masked[0], lower[...], CONTRACT_LAST, preferred_element_type=F32
    )
    by_imag = lax.dot_general(
        masked[1], lower[...], CONTRACT_LAST, preferred_element_type=F32
    )
    x_ref[0] = (by_imag[:, width:] - by_real[:, :width]).astype(BF16)
    x_ref[1] = (-(by_imag[:, :width] + by_real[:, width:])).astype(BF16)


def x_part(front, mask, owners, slots, chunk, chunks, tile):
    _, rows, cols = front.shape
    width = slots[0].shape[1] * len(slots)
    span = rows // chunks
    block = min(256, span)
    first = chunk * (span // block)
    return call(
        functools.partial(x_kernel, tile=tile, first=first),
        (span // block,),
        (mask, owners),
        [(front, pl.BlockSpec((2, block, cols), lambda j, *_: (0, first + j, 0)))]
        + [(s, whole(s.shape)) for s in slots],
        [
            (
                jax.ShapeDtypeStruct((2, span, width), BF16),
                pl.BlockSpec((2, block, width), lambda j, *_: (0, j, 0)),
            )
        ],
        [pltpu.VMEM((2, block, cols), BF16), pltpu.VMEM((2 * width, cols), BF16)],
        8 * width * span * cols,
    )[0]


def scale_kernel(pivot_ref, *rest, chunks):
    own, other, out = rest[:chunks], rest[chunks : 2 * chunks], rest[2 * chunks]
    span, width = own[0].shape[1:]
    for i in range(chunks):
        rows = slice(i * span, (i + 1) * span)
        for part in range(2):
            x = (own[i][part].astype(F32) + other[i][part].astype(F32)).astype(BF16)
            out[rows, part * width : (part + 1) * width] = (
                x.astype(F32) * pivot_ref[...]
            ).astype(BF16)


def scale(own, other, pivot):
    span, width = own[0].shape[1:]
    chunks = len(own)
    shape = (chunks * span, 2 * width)
    operands = [(pivot, whole(pivot.shape))]
    operands += [(a, whole(a.shape)) for a in (*own, *other)]
    return call(
        functools.partial(scale_kernel, chunks=chunks),
        (1,),
        (),
        operands,
        [(jax.ShapeDtypeStruct(shape, BF16), whole(shape))],
        [],
        shape[0] * shape[1] * 4,
    )[0]


def density_kernel(owners, weight, *rest, chunks):
    *slots, out, upper = rest
    parts, slots = slots[:chunks], slots[chunks:]
    assemble(owners, slots, upper)
    width = upper.shape[0] // 2
    span = parts[0].shape[1]
    shape = (2 * width, width)
    by_real, by_imag = jnp.zeros(shape, F32), jnp.zeros(shape, F32)
    for i, x in enumerate(parts):
        piece = upper[:, i * span : (i + 1) * span]
        by_real += jnp.dot(piece, x[0], preferred_element_type=F32)
        by_imag += jnp.dot(piece, x[1], preferred_element_type=F32)
    real = by_real[:width] - by_imag[width:]
    imag = by_imag[:width] + by_real[width:]
    out[...] = weight[1] * imag - weight[0] * real


def density_part(parts, owners, slots, weight):
    width = parts[0].shape[2]
    rows = slots[0].shape[2]
    shape = (width, width)
    return call(
        functools.partial(density_kernel, chunks=len(parts)),
        (1,),
        (owners, weight),
        [(a, whole(a.shape)) for a in (*parts, *slots)],
        [(jax.ShapeDtypeStruct(shape, F32), whole(shape))],
        [pltpu.VMEM((2 * width, rows), BF16)],
        8 * width * width * rows,
    )[0]


def pick_y(inner, y_mid, y_out):
    return jnp.where(inner[0] != 0, y_mid[...], y_out[...])


def update_rows(mask, scaled, y, front, new, masked, tile, col_tile):
    rows, cols = front.shape[1:]
    real, imag = y[0], y[1]
    right = jnp.concatenate(
        [
            jnp.concatenate([real, -imag], axis=0),
            jnp.concatenate([imag, real], axis=0),
        ],
        axis=1,
    )
    span = min(256, rows)
    for i in range(rows // span):
        product = jnp.dot(
            scaled[i * span : (i + 1) * span, :], right, preferred_element_type=F32
        )
        for a in range(span // tile):
            for k in range(cols // tile):
                keep = mask[i * (span // tile) + a, col_tile + k]
                factor = keep.astype(F32)
                for part in range(2):
                    at = (
                        part,
                        slice(i * span + a * tile, i * span + (a + 1) * tile),
                        slice(k * tile, (k + 1) * tile),
                    )
                    term = product[
                        a * tile : (a + 1) * tile,
                        part * cols + k * tile : part * cols + (k + 1) * tile,
                    ]
                    value = (front[at].astype(F32) + factor * term).astype(BF16)
                    new[at] = value
                    if masked is not None:
                        masked[at] = jnp.where(keep != 0, value, jnp.zeros_like(value))


def update_y_kernel(mask, owners, inner, front, scaled, y_mid, y_out, *rest, tile, first, alias):
    if alias:
        rest = rest[1:]
    *slots, new, y_ref, masked, upper = rest

    @pl.when(pl.program_id(0) == 0)
    def _():
        assemble(owners, slots, upper)

    step = first + pl.program_id(0)
    y = pick_y(inner, y_mid, y_out)
    update_rows(
        mask, scaled, y, front, new, masked, tile, step * (front.shape[2] // tile)
    )
    store_y(upper, masked, y_ref)


def update_y(front, target, mask, owners, inner, scaled, y_mid, y_out, slots, chunk, chunks, tile):
    _, rows, cols = front.shape
    width = scaled.shape[1] // 2
    span = cols // chunks
    block = min(256, span)
    first = chunk * (span // block)
    at_chunk = pl.BlockSpec((2, rows, block), lambda j, *_: (0, 0, first + j))
    in_chunk = pl.BlockSpec((2, width, block), lambda j, *_: (0, 0, j))
    operands = [
        (front, at_chunk),
        (scaled, whole(scaled.shape)),
        (y_mid, in_chunk),
        (y_out, in_chunk),
    ]
    aliases = {}
    if target is not None:
        aliases = {3 + len(operands): 0}
        operands.append((target, pl.BlockSpec(memory_space=pl.ANY)))
    operands += [(s, whole(s.shape)) for s in slots]
    return call(
        functools.partial(
            update_y_kernel, tile=tile, first=first, alias=target is not None
        ),
        (span // block,),
        (mask, owners, inner),
        operands,
        [
            (jax.ShapeDtypeStruct(front.shape, BF16), at_chunk),
            (jax.ShapeDtypeStruct((2, width, span), BF16), in_chunk),
        ],
        [pltpu.VMEM((2, rows, block), BF16), pltpu.VMEM((2 * width, rows), BF16)],
        16 * width * rows * span,
        aliases,
    )


def update_kernel(mask, inner, front, scaled, y_mid, y_out, new, *, tile, first):
    step = first + pl.program_id(0)
    y = pick_y(inner, y_mid, y_out)
    update_rows(
        mask, scaled, y, front, new, None, tile, step * (front.shape[2] // tile)
    )


def update(front, mask, inner, scaled, y_mid, y_out, chunk, chunks, tile):
    _, rows, cols = front.shape
    width = scaled.shape[1] // 2
    span = cols // chunks
    block = min(256, span)
    first = chunk * (span // block)
    at_chunk = pl.BlockSpec((2, rows, block), lambda j, *_: (0, 0, first + j))
    in_chunk = pl.BlockSpec((2, width, block), lambda j, *_: (0, 0, j))
    return call(
        functools.partial(update_kernel, tile=tile, first=first),
        (span // block,),
        (mask, inner),
        [
            (front, at_chunk),
            (scaled, whole(scaled.shape)),
            (y_mid, in_chunk),
            (y_out, in_chunk),
        ],
        [(jax.ShapeDtypeStruct(front.shape, BF16), at_chunk)],
        [],
        8 * width * rows * span,
        {2: 0},
    )[0]


def shift(value, axis, by):
    n = lax.axis_size(axis)
    return lax.ppermute(value, axis, [(i, (i + by) % n) for i in range(n)])


def gather(piece, axis):
    n = lax.axis_size(axis)
    slots = [None] * n
    slots[0] = piece
    ahead = behind = piece
    for k in range(1, n // 2 + 1):
        ahead = shift(ahead, axis, 1)
        slots[k] = ahead
        if n - k > k:
            behind = shift(behind, axis, -1)
            slots[n - k] = behind
    owners = (lax.axis_index(axis) - jnp.arange(n, dtype=jnp.int32)) % n
    return owners.astype(jnp.int32), slots


def add(left, right):
    return (left.astype(F32) + right.astype(F32)).astype(BF16)


def sum_over_row(part):
    n = lax.axis_size("row")
    if n != 4:
        total = lax.psum(part, "row")
        return total, total
    part = add(part, lax.ppermute(part, "row", [(0, 1), (3, 2)]))
    part = add(part, lax.ppermute(part, "row", [(1, 2), (2, 1)]))
    return part, lax.ppermute(part, "row", [(1, 0), (2, 3)])


def terms_over_col(part):
    if lax.axis_size("col") == 2:
        return part, shift(part, "col", 1)
    total = lax.psum(part, "col")
    return total, jnp.zeros_like(total)


def exchange_sum(value, axis):
    n = lax.axis_size(axis)
    if n & (n - 1):
        return lax.psum(value, axis)
    step = 1
    while step < n:
        partner = [(i, i ^ step) for i in range(n)]
        value = add(value, lax.ppermute(value, axis, partner))
        step *= 2
    return value


def reduce_density(part):
    n = lax.axis_size("col")
    width = part.shape[0]
    share = width // n
    narrow = part.astype(BF16)
    me = lax.axis_index("col")
    if n == 2:
        mine = lax.dynamic_slice_in_dim(narrow, me * share, share, 1)
        theirs = lax.dynamic_slice_in_dim(narrow, (1 - me) * share, share, 1)
        total = add(mine, shift(theirs, "col", 1))
    else:
        total = lax.psum_scatter(narrow, "col", scatter_dimension=1, tiled=True)
    return exchange_sum(exchange_sum(total, "pole"), "row").astype(F32)


def body(
    inverse_front, tile_mask, lower_panel, upper_panel, pivots, pole_weight, pole_slot, supernode
):
    front = inverse_front[0]
    _, rows, cols = front.shape
    width = pivots.shape[2]
    tile = rows // tile_mask.shape[0]
    chunks = 4 if min(rows, cols) % (4 * tile) == 0 else 1
    row = lax.axis_index("row")
    inner = ((row > 0) & (row < lax.axis_size("row") - 1)).astype(jnp.int32)[None]
    mine = lax.dynamic_index_in_dim(pole_slot, lax.axis_index("pole"), 0, keepdims=False)
    weight = jnp.sum(
        jnp.where(
            jnp.arange(pole_weight.shape[1], dtype=jnp.int32)[None, :] == mine, pole_weight, 0.0
        ),
        axis=1,
    )

    col_owners, upper0 = gather(upper_panel[0, 0], "col")
    row_owners, lower0 = gather(lower_panel[0, 0], "row")
    y_sums = []
    for k in range(chunks):
        y_sums.append(
            sum_over_row(y_part(front, tile_mask, col_owners, upper0, k, chunks, tile))
        )
    x_parts = [x_part(front, tile_mask, row_owners, lower0, k, chunks, tile) for k in range(chunks)]
    x_own, x_other = zip(*[terms_over_col(x) for x in x_parts])
    raw = [reduce_density(density_part(x_parts, col_owners, upper0, weight))]
    scaled = scale(x_own, x_other, pivots[0, 0][None, :])

    late_upper, late_lower, _ = lax.optimization_barrier(
        (upper_panel[1, 0], lower_panel[1, 0], y_sums[-1][0])
    )
    _, upper1 = gather(late_upper, "col")
    _, lower1 = gather(late_lower, "row")
    target = None
    next_sums = []
    for k in range(chunks):
        y_mid, y_out = y_sums[k]
        target, y = update_y(
            front, target, tile_mask, col_owners, inner, scaled, y_mid, y_out, upper1, k, chunks, tile
        )
        next_sums.append(sum_over_row(y))
    x_parts = [x_part(target, tile_mask, row_owners, lower1, k, chunks, tile) for k in range(chunks)]
    x_own, x_other = zip(*[terms_over_col(x) for x in x_parts])
    raw.append(reduce_density(density_part(x_parts, col_owners, upper1, weight)))
    scaled = scale(x_own, x_other, pivots[1, 0][None, :])
    for k in range(chunks):
        y_mid, y_out = next_sums[k]
        target = update(target, tile_mask, inner, scaled, y_mid, y_out, k, chunks, tile)

    share = width // lax.axis_size("col")
    col_start = lax.axis_index("col") * share
    results = []
    for panel in range(2):
        labels_rows = lax.dynamic_slice_in_dim(supernode, panel * width, width)
        labels_cols = lax.dynamic_slice_in_dim(supernode, panel * width + col_start, share)
        same_node = labels_rows[:, None] == labels_cols[None, :]
        results.append(jnp.where(same_node, raw[panel], jnp.zeros((), F32)))
    return target[None], jnp.stack(results)


def solution(mesh):
    in_specs = (
        P(("grp", "pole"), None, "row", "col"),
        P(("grp", "row"), "col"),
        P(None, ("grp", "pole"), None, "row", "col"),
        P(None, ("grp", "pole"), None, "col", "row"),
        P(None, ("grp", "pole"), None),
        P(None, "grp"),
        P("grp"),
        P("grp"),
    )
    out_specs = (P(("grp", "pole"), None, "row", "col"), P("grp", None, "col"))
    return jax.shard_map(body, mesh=mesh, in_specs=in_specs, out_specs=out_specs, check_vma=False)
```

```python
import functools

import jax
import jax.numpy as jnp
from jax import lax
from jax.experimental import pallas as pl
from jax.experimental.pallas import tpu as pltpu
from jax.sharding import PartitionSpec as P


F32 = jnp.float32
BF16 = jnp.bfloat16
CONTRACT_LAST = (((1,), (1,)), ((), ()))
VMEM_LIMIT = 48 << 20


def whole(shape):
    return pl.BlockSpec(
        shape, lambda *_: (0,) * len(shape), pipeline_mode=pl.Buffered(1)
    )


def call(kernel, grid, scalars, operands, outs, scratch, flops, aliases=None):
    moved = sum(a.size * a.dtype.itemsize for a, _ in operands)
    moved += sum(o.size * o.dtype.itemsize for o, _ in outs)
    shapes = [o for o, _ in outs]
    specs = [s for _, s in outs]
    return pl.pallas_call(
        kernel,
        grid_spec=pltpu.PrefetchScalarGridSpec(
            num_scalar_prefetch=len(scalars),
            grid=grid,
            in_specs=[s for _, s in operands],
            out_specs=specs,
            scratch_shapes=scratch,
        ),
        out_shape=shapes,
        input_output_aliases=aliases or {},
        compiler_params=pltpu.CompilerParams(vmem_limit_bytes=VMEM_LIMIT),
        cost_estimate=pl.CostEstimate(
            flops=flops, bytes_accessed=moved, transcendentals=0
        ),
    )(*scalars, *[a for a, _ in operands])


ANY = pl.BlockSpec(memory_space=pl.ANY)


def assemble(owners, inner, pieces, sizes, full):
    share = pieces[0].shape[1]
    width = share * len(sizes)
    at = 0
    for k, size in enumerate(sizes):
        start = pl.multiple_of(owners[k] * share, share)
        for part in range(2):
            piece = pieces[at][part]
            if size == 2:
                piece = jnp.where(inner[0] != 0, piece, pieces[at + 1][part])
            full[pl.ds(part * width + start, share), :] = piece
        at += size


def flat(slots):
    return [piece for slot in slots for piece in slot]


def sizes_of(slots):
    return tuple(len(slot) for slot in slots)


def first_step(function):
    pl.when(pl.program_id(0) == 0)(function)


def masked_tiles(mask, source, target, tile, row_tile, col_tile):
    rows, cols = source.shape[1:]
    for part in range(2):
        for i in range(rows // tile):
            for k in range(cols // tile):
                keep = mask[row_tile + i, col_tile + k] != 0
                at = (
                    part,
                    slice(i * tile, (i + 1) * tile),
                    slice(k * tile, (k + 1) * tile),
                )
                block = source[at]
                target[at] = jnp.where(keep, block, jnp.zeros_like(block))


def negative_product(upper, masked):
    width = upper.shape[0] // 2
    by_real = jnp.dot(upper, masked[0], preferred_element_type=F32)
    by_imag = jnp.dot(upper, masked[1], preferred_element_type=F32)
    return (
        (by_imag[width:] - by_real[:width]).astype(BF16),
        (-(by_imag[:width] + by_real[width:])).astype(BF16),
    )


def y_kernel(mask, order, front, *rest, tile, count):
    slots, (*outs, masked) = rest[:count], rest[count:]
    step = pl.program_id(0)
    per_piece = pl.num_programs(0) // PIECES
    block = order[step // per_piece] * per_piece + step % per_piece
    masked_tiles(mask, front, masked, tile, 0, block * (front.shape[2] // tile))
    for s, slot in enumerate(slots):
        upper = slot[...].reshape(2 * slot.shape[1], slot.shape[2])
        y = negative_product(upper, masked)
        for k in range(2):

            @pl.when(step // (2 * per_piece) == k)
            def _(y_ref=outs[2 * s + k], y=y):
                y_ref[0, 0], y_ref[0, 1] = y


def y_parts(front, mask, order, slots, tile):
    _, rows, cols = front.shape
    share = slots[0].shape[1]
    span = cols // PIECES
    block = min(256, span)
    per_piece = span // block

    def out_spec(k):
        def place(j, *_):
            at = jnp.clip(j - 2 * k * per_piece, 0, 2 * per_piece - 1)
            return (at // per_piece, 0, 0, at % per_piece)

        return pl.BlockSpec((1, 2, share, block), place)

    def column(j, mask, order):
        return (0, 0, order[j // per_piece] * per_piece + j % per_piece)

    outs = [(jax.ShapeDtypeStruct((2, 2, share, span), BF16), out_spec(k)) for k in range(2)]
    return call(
        functools.partial(y_kernel, tile=tile, count=len(slots)),
        (cols // block,),
        (mask, order),
        [(front, pl.BlockSpec((2, rows, block), column))] + [(s, whole(s.shape)) for s in slots],
        outs * len(slots),
        [pltpu.VMEM((2, rows, block), BF16)],
        8 * share * len(slots) * rows * cols,
    )


def x_kernel(mask, owners, inner, front, *rest, tile, first, sizes):
    *pieces, x_ref, masked, lower = rest

    @first_step
    def _():
        assemble(owners, inner, pieces, sizes, lower)

    step = first + pl.program_id(0)
    masked_tiles(mask, front, masked, tile, step * (front.shape[1] // tile), 0)
    width = lower.shape[0] // 2
    by_real = lax.dot_general(
        masked[0], lower[...], CONTRACT_LAST, preferred_element_type=F32
    )
    by_imag = lax.dot_general(
        masked[1], lower[...], CONTRACT_LAST, preferred_element_type=F32
    )
    x_ref[0] = (by_imag[:, width:] - by_real[:, :width]).astype(BF16)
    x_ref[1] = (-(by_imag[:, :width] + by_real[:, width:])).astype(BF16)


def x_part(front, mask, owners, inner, slots, start, span, tile):
    _, _, cols = front.shape
    width = slots[0][0].shape[1] * len(slots)
    block = min(256, span)
    first = start // block
    return call(
        functools.partial(x_kernel, tile=tile, first=first, sizes=sizes_of(slots)),
        (span // block,),
        (mask, owners, inner),
        [(front, pl.BlockSpec((2, block, cols), lambda j, *_: (0, first + j, 0)))]
        + [(s, whole(s.shape)) for s in flat(slots)],
        [
            (
                jax.ShapeDtypeStruct((2, span, width), BF16),
                pl.BlockSpec((2, block, width), lambda j, *_: (0, j, 0)),
            )
        ],
        [
            pltpu.VMEM((2, block, cols), BF16),
            pltpu.VMEM((2 * width, cols), BF16),
        ],
        8 * width * span * cols,
    )[0]


def scale(own, other, pivot):
    x = add(own, other)
    return (x.astype(F32) * pivot[None]).astype(BF16)


def density_kernel(owners, inner, weight, *rest, count, sizes):
    *pieces, out, upper = rest
    parts, pieces = pieces[:count], pieces[count:]
    assemble(owners, inner, pieces, sizes, upper)
    width = upper.shape[0] // 2
    shape = (2 * width, width)
    by_real, by_imag = jnp.zeros(shape, F32), jnp.zeros(shape, F32)
    start = 0
    for x in parts:
        piece = upper[:, start : start + x.shape[1]]
        start += x.shape[1]
        by_real += jnp.dot(piece, x[0], preferred_element_type=F32)
        by_imag += jnp.dot(piece, x[1], preferred_element_type=F32)
    real = by_real[:width] - by_imag[width:]
    imag = by_imag[:width] + by_real[width:]
    out[...] = (weight[1] * imag - weight[0] * real).astype(BF16)


def density_part(parts, owners, inner, slots, weight):
    width = parts[0].shape[2]
    rows = slots[0][0].shape[2]
    shape = (width, width)
    return call(
        functools.partial(density_kernel, count=len(parts), sizes=sizes_of(slots)),
        (1,),
        (owners, inner, weight),
        [(a, whole(a.shape)) for a in (*parts, *flat(slots))],
        [(jax.ShapeDtypeStruct(shape, BF16), whole(shape))],
        [pltpu.VMEM((2 * width, rows), BF16)],
        8 * width * width * rows,
    )[0]


def fill_right(right, start, real, imag):
    width, cols = right.shape[0] // 2, right.shape[1] // 2
    share = real.shape[0]
    right[pl.ds(start, share), :cols] = real
    right[pl.ds(start, share), cols:] = imag
    right[pl.ds(width + start, share), :cols] = -imag
    right[pl.ds(width + start, share), cols:] = real


def update_rows(mask, scaled, right, front, new, masked, tile, row_tile, col_tile):
    _, cols = front.shape[1:]
    span = min(256, *[left.shape[1] for left in scaled])
    blocks = [(left, at) for left in scaled for at in range(0, left.shape[1], span)]
    for i, (left, start) in enumerate(blocks):
        at_left = slice(start, start + span)
        both = jnp.concatenate([left[0, at_left, :], left[1, at_left, :]], axis=1)
        product = jnp.dot(both, right[...], preferred_element_type=F32)
        for a in range(span // tile):
            for k in range(cols // tile):
                keep = mask[row_tile + i * (span // tile) + a, col_tile + k]
                factor = keep.astype(F32)
                for part in range(2):
                    at = (
                        part,
                        slice(i * span + a * tile, i * span + (a + 1) * tile),
                        slice(k * tile, (k + 1) * tile),
                    )
                    term = product[
                        a * tile : (a + 1) * tile,
                        part * cols + k * tile : part * cols + (k + 1) * tile,
                    ]
                    value = (front[at].astype(F32) + factor * term).astype(BF16)
                    new[at] = value
                    if masked is not None:
                        masked[at] = jnp.where(keep != 0, value, jnp.zeros_like(value))


def update_y_kernel(mask, owners, inner, order, front, y, *rest, tile, piece, parts, alias, sizes):
    scaled, rest = rest[:parts], rest[parts + alias :]
    *gathered, new, y_ref, masked, right, upper = rest

    @first_step
    def _():
        assemble(owners, inner, gathered, sizes, upper)

    for k in range(y.shape[0]):
        share = y.shape[2]
        fill_right(right, pl.multiple_of(owners[k] * share, share), y[k, 0], y[k, 1])
    block = order[piece] * pl.num_programs(0) + pl.program_id(0)
    update_rows(
        mask, scaled, right, front, new, masked, tile, 0, block * (front.shape[2] // tile)
    )
    y_ref[0], y_ref[1] = negative_product(upper[...], masked)


def update_y(front, target, mask, owners, inner, order, scaled, y, slots, piece, tile):
    _, rows, cols = front.shape
    share = slots[0][0].shape[1]
    width = share * len(slots)
    span = cols // PIECES
    block = min(256, span)
    per_piece = span // block

    def column(j, mask, owners, inner, order):
        return (0, 0, order[piece] * per_piece + j)

    at_piece = pl.BlockSpec((2, rows, block), column)
    term = pl.BlockSpec((*y.shape[:3], block), lambda j, *_: (0, 0, 0, j))
    operands = [(front, at_piece), (y, term)]
    operands += [(s, whole(s.shape)) for s in scaled]
    aliases = {}
    if target is not None:
        aliases = {4 + len(operands): 0}
        operands.append((target, ANY))
    operands += [(s, whole(s.shape)) for s in flat(slots)]
    return call(
        functools.partial(
            update_y_kernel,
            tile=tile,
            piece=piece,
            parts=len(scaled),
            alias=int(target is not None),
            sizes=sizes_of(slots),
        ),
        (per_piece,),
        (mask, owners, inner, order),
        operands,
        [
            (jax.ShapeDtypeStruct(front.shape, BF16), at_piece),
            (
                jax.ShapeDtypeStruct((2, width, span), BF16),
                pl.BlockSpec((2, width, block), lambda j, *_: (0, 0, j)),
            ),
        ],
        [
            pltpu.VMEM((2, rows, block), BF16),
            pltpu.VMEM((2 * width, 2 * block), BF16),
            pltpu.VMEM((2 * width, rows), BF16),
        ],
        16 * width * rows * span,
        aliases,
    )


def update_kernel(mask, order, front, y, *rest, tile, piece):
    *scaled, new, right = rest
    fill_right(right, 0, y[0], y[1])
    block = order[piece] * pl.num_programs(0) + pl.program_id(0)
    col_tile = block * (front.shape[2] // tile)
    update_rows(mask, scaled, right, front, new, None, tile, 0, col_tile)


def update(front, mask, order, scaled, y, piece, tile):
    _, rows, cols = front.shape
    width = scaled[0].shape[2]
    span = cols // PIECES
    block = min(256, span)
    per_piece = span // block

    def column(j, mask, order):
        return (0, 0, order[piece] * per_piece + j)

    at_piece = pl.BlockSpec((2, rows, block), column)
    return call(
        functools.partial(update_kernel, tile=tile, piece=piece),
        (per_piece,),
        (mask, order),
        [(front, at_piece), (y, pl.BlockSpec((2, width, block), lambda j, *_: (0, 0, j)))]
        + [(s, whole(s.shape)) for s in scaled],
        [(jax.ShapeDtypeStruct(front.shape, BF16), at_piece)],
        [pltpu.VMEM((2 * width, 2 * block), BF16)],
        8 * width * rows * span,
        {2: 0},
    )[0]


def shift(value, axis, by):
    n = lax.axis_size(axis)
    return lax.ppermute(value, axis, [(i, (i + by) % n) for i in range(n)])


def gather(piece, axis):
    n = lax.axis_size(axis)
    slots = [None] * n
    slots[0] = (piece,)
    ahead = behind = piece
    for k in range(1, n // 2 + 1):
        ahead = shift(ahead, axis, 1)
        slots[k] = (ahead,)
        if n - k > k:
            behind = shift(behind, axis, -1)
            slots[n - k] = (behind,)
    owners = (lax.axis_index(axis) - jnp.arange(n, dtype=jnp.int32)) % n
    return owners.astype(jnp.int32), slots


def gather_line(piece, axis):
    n = lax.axis_size(axis)
    if n != 4:
        return gather(piece, axis)
    swap, across, outward = [(0, 1), (1, 0), (2, 3), (3, 2)], [(1, 2), (2, 1)], [(1, 0), (2, 3)]
    near = lax.ppermute(piece, axis, swap)
    mid0 = lax.ppermute(piece, axis, across)
    mid1 = lax.ppermute(near, axis, across)
    out0 = lax.ppermute(mid0, axis, outward)
    out1 = lax.ppermute(mid1, axis, outward)
    me = lax.axis_index(axis)
    first = jnp.where(me < 2, 2, 1)
    owners = jnp.stack([me, me ^ 1, first, first ^ 1]).astype(jnp.int32)
    return owners, [(piece,), (near,), (mid0, out0), (mid1, out1)]


def add(left, right):
    return (left.astype(F32) + right.astype(F32)).astype(BF16)


def flip(value, bit):
    pairs = [(i, i ^ bit) for i in range(lax.axis_size("row"))]
    return lax.ppermute(value, "row", pairs)


def add3(one, two, three):
    return (one.astype(F32) + two.astype(F32) + three.astype(F32)).astype(BF16)


def stacked(function, *lists):
    return jnp.stack([function(*terms) for terms in zip(*lists)])


def spread(own):
    near = flip(own, 1)
    far = flip(own, 2)
    return [near, flip(far, 1), far, own]


def sum_first(terms):
    sent, kept = terms[0::2], terms[1::2]
    if lax.axis_size("row") != 4:
        sums = [lax.psum(jnp.concatenate(pair), "row") for pair in zip(sent, kept)]
        return [jnp.stack([total[k] for total in sums]) for k in range(PIECES)]
    got = [flip(y, 1) for y in sent]
    passed = stacked(add, [k[0] for k in kept], [g[1] for g in got])
    other = flip(passed, 2)
    own = stacked(add3, [k[1] for k in kept], [g[0] for g in got], list(other))
    return spread(own)


def sum_next(terms):
    if lax.axis_size("row") != 4:
        return [lax.psum(y, "row") for y in terms]
    got = [flip(y, 1) for y in terms[:2]]
    passed = add(terms[2], got[1])
    other = flip(passed, 2)
    own = add3(terms[3], got[0], other)
    return spread(own)


def terms_over_col(part):
    if lax.axis_size("col") == 2:
        return part, shift(part, "col", 1)
    total = lax.psum(part, "col")
    return total, jnp.zeros_like(total)


def exchange_sum(value, axis):
    n = lax.axis_size(axis)
    if n & (n - 1):
        return lax.psum(value, axis)
    step = 1
    while step < n:
        partner = [(i, i ^ step) for i in range(n)]
        other = lax.ppermute(value, axis, partner)
        value = add(value, other)
        step *= 2
    return value


def reduce_density(part):
    n = lax.axis_size("col")
    share = part.shape[2] // n
    narrow = part
    me = lax.axis_index("col")
    if n == 2:
        mine = lax.dynamic_slice_in_dim(narrow, me * share, share, 2)
        theirs = lax.dynamic_slice_in_dim(narrow, (1 - me) * share, share, 2)
        total = add(mine, shift(theirs, "col", 1))
    else:
        total = lax.psum_scatter(narrow, "col", scatter_dimension=2, tiled=True)
    total = exchange_sum(total, "pole")
    return exchange_sum(total, "row").astype(F32)


def body(
    inverse_front, tile_mask, lower_panel, upper_panel, pivots, pole_weight, pole_slot, supernode
):
    front = inverse_front[0]
    _, rows, _ = front.shape
    width = pivots.shape[2]
    tile = rows // tile_mask.shape[0]
    me = lax.axis_index("row")
    order = jnp.arange(PIECES, dtype=jnp.int32)
    if lax.axis_size("row") == 4:
        order = jnp.stack([me ^ 1, me ^ 3, me ^ 2, me]).astype(jnp.int32)
    unit = rows // 4 if rows % (4 * tile) == 0 else rows
    parts = {panel: [(a * unit, b * unit) for a, b in PARTS[panel]] for panel in range(2)}
    if unit == rows:
        parts = {panel: [(0, rows)] for panel in range(2)}
    row = lax.axis_index("row")
    inner = ((row > 0) & (row < lax.axis_size("row") - 1)).astype(jnp.int32)[None]
    mine = lax.dynamic_index_in_dim(pole_slot, lax.axis_index("pole"), 0, keepdims=False)
    weight = jnp.sum(
        jnp.where(
            jnp.arange(pole_weight.shape[1], dtype=jnp.int32)[None, :] == mine, pole_weight, 0.0
        ),
        axis=1,
    )

    def x_phase(front, slots, panel):
        terms = [
            x_part(front, tile_mask, row_owners, inner, slots, *at, tile)
            for at in parts[panel]
        ]
        pairs = [terms_over_col(x) for x in terms]
        scaled = [scale(one, two, pivots[panel, 0][None, :]) for one, two in pairs]
        return terms, scaled

    row_owners, lower0 = gather_line(lower_panel[0, 0], "row")
    col_owners, upper0 = gather(upper_panel[0, 0], "col")
    _, upper1 = gather(upper_panel[1, 0], "col")
    _, lower1 = gather_line(lower_panel[1, 0], "row")
    y_terms = y_parts(front, tile_mask, order, flat(upper0[:1]), tile)
    y_terms += y_parts(front, tile_mask, order, flat(upper0[1:]), tile)
    y_sums = sum_first(y_terms)
    terms0, scaled = x_phase(front, lower0, 0)

    target = None
    y_terms = [None] * PIECES
    for k in UPDATES:
        target, y_terms[k] = update_y(
            front, target, tile_mask, col_owners, inner, order, scaled,
            y_sums[k], upper1, k, tile,
        )
    y_sums = sum_next(y_terms)
    terms1, scaled = x_phase(target, lower1, 1)
    raw0 = density_part(terms0, col_owners, inner, upper0, weight)
    raw1 = density_part(terms1, col_owners, inner, upper1, weight)
    raw = reduce_density(jnp.stack([raw0, raw1]))
    for k in LAST_UPDATES:
        target = update(target, tile_mask, order, scaled, y_sums[k], k, tile)

    share = width // lax.axis_size("col")
    col_start = lax.axis_index("col") * share
    results = []
    for panel in range(2):
        labels_rows = lax.dynamic_slice_in_dim(supernode, panel * width, width)
        labels_cols = lax.dynamic_slice_in_dim(supernode, panel * width + col_start, share)
        same_node = labels_rows[:, None] == labels_cols[None, :]
        results.append(jnp.where(same_node, raw[panel], jnp.zeros((), F32)))
    return target[None], jnp.stack(results)


PIECES = 4
UPDATES = (3, 0, 2, 1)
LAST_UPDATES = (3, 0, 2, 1)
PARTS = (((0, 2), (2, 2)), ((0, 2), (2, 1), (3, 1)))


def solution(mesh):
    in_specs = (
        P(("grp", "pole"), None, "row", "col"),
        P(("grp", "row"), "col"),
        P(None, ("grp", "pole"), None, "row", "col"),
        P(None, ("grp", "pole"), None, "col", "row"),
        P(None, ("grp", "pole"), None),
        P(None, "grp"),
        P("grp"),
        P("grp"),
    )
    out_specs = (P(("grp", "pole"), None, "row", "col"), P("grp", None, "col"))

    return jax.shard_map(body, mesh=mesh, in_specs=in_specs, out_specs=out_specs, check_vma=False)
```

```python
import functools

import jax
import jax.numpy as jnp
from jax import lax
from jax.experimental import pallas as pl
from jax.experimental.pallas import tpu as pltpu
from jax.sharding import PartitionSpec as P


F32 = jnp.float32
BF16 = jnp.bfloat16
CONTRACT_LAST = (((1,), (1,)), ((), ()))
VMEM_LIMIT = 48 << 20


def whole(shape):
    return pl.BlockSpec(
        shape, lambda *_: (0,) * len(shape), pipeline_mode=pl.Buffered(1)
    )


def call(kernel, grid, scalars, operands, outs, scratch, flops, aliases=None):
    moved = sum(a.size * a.dtype.itemsize for a, _ in operands)
    moved += sum(o.size * o.dtype.itemsize for o, _ in outs)
    shapes = [o for o, _ in outs]
    specs = [s for _, s in outs]
    return pl.pallas_call(
        kernel,
        grid_spec=pltpu.PrefetchScalarGridSpec(
            num_scalar_prefetch=len(scalars),
            grid=grid,
            in_specs=[s for _, s in operands],
            out_specs=specs,
            scratch_shapes=scratch,
        ),
        out_shape=shapes,
        input_output_aliases=aliases or {},
        compiler_params=pltpu.CompilerParams(vmem_limit_bytes=VMEM_LIMIT),
        cost_estimate=pl.CostEstimate(
            flops=flops, bytes_accessed=moved, transcendentals=0
        ),
    )(*scalars, *[a for a, _ in operands])


ANY = pl.BlockSpec(memory_space=pl.ANY)


def assemble(owners, inner, pieces, sizes, full):
    share = pieces[0].shape[1]
    width = share * len(sizes)
    at = 0
    for k, size in enumerate(sizes):
        start = pl.multiple_of(owners[k] * share, share)
        for part in range(2):
            piece = pieces[at][part]
            if size == 2:
                piece = jnp.where(inner[0] != 0, piece, pieces[at + 1][part])
            full[pl.ds(part * width + start, share), :] = piece
        at += size


def flat(slots):
    return [piece for slot in slots for piece in slot]


def sizes_of(slots):
    return tuple(len(slot) for slot in slots)


def first_step(function):
    pl.when(pl.program_id(0) == 0)(function)


def masked_tiles(mask, source, target, tile, row_tile, col_tile):
    rows, cols = source.shape[1:]
    for part in range(2):
        for i in range(rows // tile):
            for k in range(cols // tile):
                keep = mask[row_tile + i, col_tile + k] != 0
                at = (
                    part,
                    slice(i * tile, (i + 1) * tile),
                    slice(k * tile, (k + 1) * tile),
                )
                block = source[at]
                target[at] = jnp.where(keep, block, jnp.zeros_like(block))


def negative_product(upper, masked):
    width = upper.shape[0] // 2
    by_real = jnp.dot(upper, masked[0], preferred_element_type=F32)
    by_imag = jnp.dot(upper, masked[1], preferred_element_type=F32)
    return (
        (by_imag[width:] - by_real[:width]).astype(BF16),
        (-(by_imag[:width] + by_real[width:])).astype(BF16),
    )


def y_kernel(mask, order, front, *rest, tile, half):
    *slots_outs, masked = rest
    count = len(slots_outs) // 2
    slots, outs = slots_outs[:count], slots_outs[count:]
    per_piece = pl.num_programs(0) // 2
    step = pl.program_id(0)
    block = order[2 * half + step // per_piece] * per_piece + step % per_piece
    masked_tiles(mask, front, masked, tile, 0, block * (front.shape[2] // tile))
    for slot, y_ref in zip(slots, outs):
        upper = slot[...].reshape(2 * slot.shape[1], slot.shape[2])
        y_ref[0, 0], y_ref[0, 1] = negative_product(upper, masked)


def y_part(front, mask, order, slots, half, tile):
    _, rows, cols = front.shape
    share = slots[0].shape[1]
    span = cols // PIECES
    block = min(256, span)
    per_piece = span // block

    def column(j, mask, order):
        return (0, 0, order[2 * half + j // per_piece] * per_piece + j % per_piece)

    out = (
        jax.ShapeDtypeStruct((2, 2, share, span), BF16),
        pl.BlockSpec((1, 2, share, block), lambda j, *_: (j // per_piece, 0, 0, j % per_piece)),
    )
    return call(
        functools.partial(y_kernel, tile=tile, half=half),
        (2 * per_piece,),
        (mask, order),
        [(front, pl.BlockSpec((2, rows, block), column))] + [(s, whole(s.shape)) for s in slots],
        [out] * len(slots),
        [pltpu.VMEM((2, rows, block), BF16)],
        4 * share * len(slots) * rows * cols,
    )


def x_kernel(mask, owners, inner, front, *rest, tile, first, sizes):
    *pieces, x_ref, masked, lower = rest

    @first_step
    def _():
        assemble(owners, inner, pieces, sizes, lower)

    step = first + pl.program_id(0)
    masked_tiles(mask, front, masked, tile, step * (front.shape[1] // tile), 0)
    width = lower.shape[0] // 2
    by_real = lax.dot_general(
        masked[0], lower[...], CONTRACT_LAST, preferred_element_type=F32
    )
    by_imag = lax.dot_general(
        masked[1], lower[...], CONTRACT_LAST, preferred_element_type=F32
    )
    x_ref[0] = (by_imag[:, width:] - by_real[:, :width]).astype(BF16)
    x_ref[1] = (-(by_imag[:, :width] + by_real[:, width:])).astype(BF16)


def x_part(front, mask, owners, inner, slots, start, span, tile):
    _, _, cols = front.shape
    width = slots[0][0].shape[1] * len(slots)
    block = min(256, span)
    first = start // block
    return call(
        functools.partial(x_kernel, tile=tile, first=first, sizes=sizes_of(slots)),
        (span // block,),
        (mask, owners, inner),
        [(front, pl.BlockSpec((2, block, cols), lambda j, *_: (0, first + j, 0)))]
        + [(s, whole(s.shape)) for s in flat(slots)],
        [
            (
                jax.ShapeDtypeStruct((2, span, width), BF16),
                pl.BlockSpec((2, block, width), lambda j, *_: (0, j, 0)),
            )
        ],
        [
            pltpu.VMEM((2, block, cols), BF16),
            pltpu.VMEM((2 * width, cols), BF16),
        ],
        8 * width * span * cols,
    )[0]


def scale(own, other, pivot):
    x = add(own, other)
    return (x.astype(F32) * pivot[None]).astype(BF16)


def density_kernel(owners, inner, weight, *rest, count, sizes):
    *pieces, out, upper = rest
    parts, pieces = pieces[:count], pieces[count:]
    assemble(owners, inner, pieces, sizes, upper)
    width = upper.shape[0] // 2
    shape = (2 * width, width)
    by_real, by_imag = jnp.zeros(shape, F32), jnp.zeros(shape, F32)
    start = 0
    for x in parts:
        piece = upper[:, start : start + x.shape[1]]
        start += x.shape[1]
        by_real += jnp.dot(piece, x[0], preferred_element_type=F32)
        by_imag += jnp.dot(piece, x[1], preferred_element_type=F32)
    real = by_real[:width] - by_imag[width:]
    imag = by_imag[:width] + by_real[width:]
    out[...] = (weight[1] * imag - weight[0] * real).astype(BF16)


def density_part(parts, owners, inner, slots, weight):
    width = parts[0].shape[2]
    rows = slots[0][0].shape[2]
    shape = (width, width)
    return call(
        functools.partial(density_kernel, count=len(parts), sizes=sizes_of(slots)),
        (1,),
        (owners, inner, weight),
        [(a, whole(a.shape)) for a in (*parts, *flat(slots))],
        [(jax.ShapeDtypeStruct(shape, BF16), whole(shape))],
        [pltpu.VMEM((2 * width, rows), BF16)],
        8 * width * width * rows,
    )[0]


def fill_right(right, start, real, imag):
    width, cols = right.shape[0] // 2, right.shape[1] // 2
    share = real.shape[0]
    right[pl.ds(start, share), :cols] = real
    right[pl.ds(start, share), cols:] = imag
    right[pl.ds(width + start, share), :cols] = -imag
    right[pl.ds(width + start, share), cols:] = real


def update_rows(mask, scaled, right, front, new, masked, tile, row_tile, col_tile):
    _, cols = front.shape[1:]
    span = min(256, *[left.shape[1] for left in scaled])
    blocks = [(left, at) for left in scaled for at in range(0, left.shape[1], span)]
    for i, (left, start) in enumerate(blocks):
        at_left = slice(start, start + span)
        both = jnp.concatenate([left[0, at_left, :], left[1, at_left, :]], axis=1)
        product = jnp.dot(both, right[...], preferred_element_type=F32)
        for a in range(span // tile):
            for k in range(cols // tile):
                keep = mask[row_tile + i * (span // tile) + a, col_tile + k]
                factor = keep.astype(F32)
                for part in range(2):
                    at = (
                        part,
                        slice(i * span + a * tile, i * span + (a + 1) * tile),
                        slice(k * tile, (k + 1) * tile),
                    )
                    term = product[
                        a * tile : (a + 1) * tile,
                        part * cols + k * tile : part * cols + (k + 1) * tile,
                    ]
                    value = (front[at].astype(F32) + factor * term).astype(BF16)
                    new[at] = value
                    if masked is not None:
                        masked[at] = jnp.where(keep != 0, value, jnp.zeros_like(value))


def update_y_kernel(mask, owners, inner, order, front, y, *rest, tile, piece, parts, alias, sizes):
    scaled, rest = rest[:parts], rest[parts + alias :]
    *gathered, new, y_ref, masked, right, upper = rest

    @first_step
    def _():
        assemble(owners, inner, gathered, sizes, upper)

    for k in range(y.shape[0]):
        share = y.shape[2]
        fill_right(right, pl.multiple_of(owners[k] * share, share), y[k, 0], y[k, 1])
    block = order[piece] * pl.num_programs(0) + pl.program_id(0)
    update_rows(
        mask, scaled, right, front, new, masked, tile, 0, block * (front.shape[2] // tile)
    )
    y_ref[0], y_ref[1] = negative_product(upper[...], masked)


def update_y(front, target, mask, owners, inner, order, scaled, y, slots, piece, tile):
    _, rows, cols = front.shape
    share = slots[0][0].shape[1]
    width = share * len(slots)
    span = cols // PIECES
    block = min(256, span)
    per_piece = span // block

    def column(j, mask, owners, inner, order):
        return (0, 0, order[piece] * per_piece + j)

    at_piece = pl.BlockSpec((2, rows, block), column)
    term = pl.BlockSpec((*y.shape[:3], block), lambda j, *_: (0, 0, 0, j))
    operands = [(front, at_piece), (y, term)]
    operands += [(s, whole(s.shape)) for s in scaled]
    aliases = {}
    if target is not None:
        aliases = {4 + len(operands): 0}
        operands.append((target, ANY))
    operands += [(s, whole(s.shape)) for s in flat(slots)]
    return call(
        functools.partial(
            update_y_kernel,
            tile=tile,
            piece=piece,
            parts=len(scaled),
            alias=int(target is not None),
            sizes=sizes_of(slots),
        ),
        (per_piece,),
        (mask, owners, inner, order),
        operands,
        [
            (jax.ShapeDtypeStruct(front.shape, BF16), at_piece),
            (
                jax.ShapeDtypeStruct((2, width, span), BF16),
                pl.BlockSpec((2, width, block), lambda j, *_: (0, 0, j)),
            ),
        ],
        [
            pltpu.VMEM((2, rows, block), BF16),
            pltpu.VMEM((2 * width, 2 * block), BF16),
            pltpu.VMEM((2 * width, rows), BF16),
        ],
        16 * width * rows * span,
        aliases,
    )


def update_kernel(mask, order, front, y, *rest, tile, piece):
    *scaled, new, right = rest
    fill_right(right, 0, y[0], y[1])
    block = order[piece] * pl.num_programs(0) + pl.program_id(0)
    col_tile = block * (front.shape[2] // tile)
    update_rows(mask, scaled, right, front, new, None, tile, 0, col_tile)


def update(front, mask, order, scaled, y, piece, tile):
    _, rows, cols = front.shape
    width = scaled[0].shape[2]
    span = cols // PIECES
    block = min(256, span)
    per_piece = span // block

    def column(j, mask, order):
        return (0, 0, order[piece] * per_piece + j)

    at_piece = pl.BlockSpec((2, rows, block), column)
    return call(
        functools.partial(update_kernel, tile=tile, piece=piece),
        (per_piece,),
        (mask, order),
        [(front, at_piece), (y, pl.BlockSpec((2, width, block), lambda j, *_: (0, 0, j)))]
        + [(s, whole(s.shape)) for s in scaled],
        [(jax.ShapeDtypeStruct(front.shape, BF16), at_piece)],
        [pltpu.VMEM((2 * width, 2 * block), BF16)],
        8 * width * rows * span,
        {2: 0},
    )[0]


def shift(value, axis, by):
    n = lax.axis_size(axis)
    return lax.ppermute(value, axis, [(i, (i + by) % n) for i in range(n)])


def gather(piece, axis):
    n = lax.axis_size(axis)
    slots = [None] * n
    slots[0] = (piece,)
    ahead = behind = piece
    for k in range(1, n // 2 + 1):
        ahead = shift(ahead, axis, 1)
        slots[k] = (ahead,)
        if n - k > k:
            behind = shift(behind, axis, -1)
            slots[n - k] = (behind,)
    owners = (lax.axis_index(axis) - jnp.arange(n, dtype=jnp.int32)) % n
    return owners.astype(jnp.int32), slots


def gather_line(piece, axis):
    n = lax.axis_size(axis)
    if n != 4:
        return gather(piece, axis)
    swap, across, outward = [(0, 1), (1, 0), (2, 3), (3, 2)], [(1, 2), (2, 1)], [(1, 0), (2, 3)]
    near = lax.ppermute(piece, axis, swap)
    mid0 = lax.ppermute(piece, axis, across)
    mid1 = lax.ppermute(near, axis, across)
    out0 = lax.ppermute(mid0, axis, outward)
    out1 = lax.ppermute(mid1, axis, outward)
    me = lax.axis_index(axis)
    first = jnp.where(me < 2, 2, 1)
    owners = jnp.stack([me, me ^ 1, first, first ^ 1]).astype(jnp.int32)
    return owners, [(piece,), (near,), (mid0, out0), (mid1, out1)]


def add(left, right):
    return (left.astype(F32) + right.astype(F32)).astype(BF16)


def flip(value, bit):
    pairs = [(i, i ^ bit) for i in range(lax.axis_size("row"))]
    return lax.ppermute(value, "row", pairs)


def add3(one, two, three):
    return (one.astype(F32) + two.astype(F32) + three.astype(F32)).astype(BF16)


def stacked(function, *lists):
    return jnp.stack([function(*terms) for terms in zip(*lists)])


def spread(own):
    near = flip(own, 1)
    far = flip(own, 2)
    return [near, flip(far, 1), far, own]


def sum_first(sent, kept):
    if lax.axis_size("row") != 4:
        sums = [lax.psum(jnp.concatenate(pair), "row") for pair in zip(sent, kept)]
        return [jnp.stack([total[k] for total in sums]) for k in range(PIECES)]
    got = [flip(y, 1) for y in sent]
    passed = stacked(add, [k[0] for k in kept], [g[1] for g in got])
    other = flip(passed, 2)
    own = stacked(add3, [k[1] for k in kept], [g[0] for g in got], list(other))
    return spread(own)


def sum_next(terms):
    if lax.axis_size("row") != 4:
        return [lax.psum(y, "row") for y in terms]
    got = [flip(y, 1) for y in terms[:2]]
    passed = add(terms[2], got[1])
    other = flip(passed, 2)
    own = add3(terms[3], got[0], other)
    return spread(own)


def terms_over_col(part):
    if lax.axis_size("col") == 2:
        return part, shift(part, "col", 1)
    total = lax.psum(part, "col")
    return total, jnp.zeros_like(total)


def exchange_sum(value, axis):
    n = lax.axis_size(axis)
    if n & (n - 1):
        return lax.psum(value, axis)
    step = 1
    while step < n:
        partner = [(i, i ^ step) for i in range(n)]
        other = lax.ppermute(value, axis, partner)
        value = add(value, other)
        step *= 2
    return value


def reduce_density(part):
    n = lax.axis_size("col")
    share = part.shape[2] // n
    narrow = part
    me = lax.axis_index("col")
    if n == 2:
        mine = lax.dynamic_slice_in_dim(narrow, me * share, share, 2)
        theirs = lax.dynamic_slice_in_dim(narrow, (1 - me) * share, share, 2)
        total = add(mine, shift(theirs, "col", 1))
    else:
        total = lax.psum_scatter(narrow, "col", scatter_dimension=2, tiled=True)
    total = exchange_sum(total, "pole")
    return exchange_sum(total, "row").astype(F32)


def body(
    inverse_front, tile_mask, lower_panel, upper_panel, pivots, pole_weight, pole_slot, supernode
):
    front = inverse_front[0]
    _, rows, _ = front.shape
    width = pivots.shape[2]
    tile = rows // tile_mask.shape[0]
    me = lax.axis_index("row")
    order = jnp.arange(PIECES, dtype=jnp.int32)
    if lax.axis_size("row") == 4:
        order = jnp.stack([me ^ 1, me ^ 3, me ^ 2, me]).astype(jnp.int32)
    unit = rows // 4 if rows % (4 * tile) == 0 else rows
    parts = {panel: [(a * unit, b * unit) for a, b in PARTS[panel]] for panel in range(2)}
    if unit == rows:
        parts = {panel: [(0, rows)] for panel in range(2)}
    row = lax.axis_index("row")
    inner = ((row > 0) & (row < lax.axis_size("row") - 1)).astype(jnp.int32)[None]
    mine = lax.dynamic_index_in_dim(pole_slot, lax.axis_index("pole"), 0, keepdims=False)
    weight = jnp.sum(
        jnp.where(
            jnp.arange(pole_weight.shape[1], dtype=jnp.int32)[None, :] == mine, pole_weight, 0.0
        ),
        axis=1,
    )

    def x_phase(front, slots, panel):
        terms = [
            x_part(front, tile_mask, row_owners, inner, slots, *at, tile)
            for at in parts[panel]
        ]
        pairs = [terms_over_col(x) for x in terms]
        scaled = [scale(one, two, pivots[panel, 0][None, :]) for one, two in pairs]
        return terms, scaled

    row_owners, lower0 = gather_line(lower_panel[0, 0], "row")
    col_owners, upper0 = gather(upper_panel[0, 0], "col")
    _, upper1 = gather(upper_panel[1, 0], "col")
    _, lower1 = gather_line(lower_panel[1, 0], "row")
    halves = []
    for half in range(2):
        terms = []
        for slots in (upper0[:1], upper0[1:]):
            terms += y_part(front, tile_mask, order, flat(slots), half, tile)
        halves.append(terms)
    y_sums = sum_first(*halves)
    terms0, scaled = x_phase(front, lower0, 0)

    target = None
    y_terms = [None] * PIECES
    for k in UPDATES:
        target, y_terms[k] = update_y(
            front, target, tile_mask, col_owners, inner, order, scaled,
            y_sums[k], upper1, k, tile,
        )
    y_sums = sum_next(y_terms)
    terms1, scaled = x_phase(target, lower1, 1)
    raw0 = density_part(terms0, col_owners, inner, upper0, weight)
    raw1 = density_part(terms1, col_owners, inner, upper1, weight)
    raw = reduce_density(jnp.stack([raw0, raw1]))
    for k in LAST_UPDATES:
        target = update(target, tile_mask, order, scaled, y_sums[k], k, tile)

    share = width // lax.axis_size("col")
    col_start = lax.axis_index("col") * share
    results = []
    for panel in range(2):
        labels_rows = lax.dynamic_slice_in_dim(supernode, panel * width, width)
        labels_cols = lax.dynamic_slice_in_dim(supernode, panel * width + col_start, share)
        same_node = labels_rows[:, None] == labels_cols[None, :]
        results.append(jnp.where(same_node, raw[panel], jnp.zeros((), F32)))
    return target[None], jnp.stack(results)


PIECES = 4
UPDATES = (3, 0, 2, 1)
LAST_UPDATES = (3, 0, 2, 1)
PARTS = (((0, 2), (2, 2)), ((0, 2), (2, 1), (3, 1)))


def solution(mesh):
    in_specs = (
        P(("grp", "pole"), None, "row", "col"),
        P(("grp", "row"), "col"),
        P(None, ("grp", "pole"), None, "row", "col"),
        P(None, ("grp", "pole"), None, "col", "row"),
        P(None, ("grp", "pole"), None),
        P(None, "grp"),
        P("grp"),
        P("grp"),
    )
    out_specs = (P(("grp", "pole"), None, "row", "col"), P("grp", None, "col"))

    return jax.shard_map(body, mesh=mesh, in_specs=in_specs, out_specs=out_specs, check_vma=False)
```
